32 devices in a mesh: dom: 32 (over z, y, x, core).
Axes of the slice: x: 2, y: 2, z: 4, core: 2. Of those that a mesh axis runs over, the one named last changes fastest.
Arguments:
- features: bfloat16 [262144, 128], P('dom'), may hold values from -6 to 6
- labels: int32 [65536], P('dom'), may hold values from 0 to 171
- seed_count: int32 [32], P('dom'), may hold values from 1024 to 2048, as said below
- src1: int32 [65536, 15], P('dom'), may hold values from -1 to 8191, as said below
- cnt1: int32 [65536], P('dom'), may hold values from 0 to 15, as said below
- dst1: int32 [65536], P('dom'), may hold values from 0 to 8191
- src2: int32 [16384, 10], P('dom'), may hold values from -1 to 8191, as said below
- cnt2: int32 [16384], P('dom'), may hold values from 0 to 10, as said below
- dst2: int32 [16384], P('dom'), may hold values from 0 to 2047
- master: float32 [155648], P('dom')
- moment1: float32 [155648], P('dom'), may hold values from -0.046875 to 0.046875
- moment2: float32 [155648], P('dom'), may hold values from 1e-06 to 0.0001
Outputs:
- loss: float32 [], replicated
- new_master: float32 [155648], P('dom')
- new_moment1: float32 [155648], P('dom')
- new_moment2: float32 [155648], P('dom')
The draws below stay inside these ranges and needn't reach their ends.
Inputs may be any that keep to these rules, and one draw needn't show every extreme that they name: `seed_count`: each trainer has between 1024 and 2048 live seeds; some trainer has exactly 2048. `src1`: in each slot the first cnt entries are source rows and the rest are -1; an empty slot has all -1; some slot is full. From one owner to one device at most 32 slots are non-empty, and some owner sends exactly 32 to some device; which slots are non-empty varies. `cnt1`: equals the number of non-negative entries of the matching src1 slot. `src2`: in each slot the first cnt entries are source rows and the rest are -1; an empty slot has all -1; some slot is full. From one owner to one trainer at most 8 slots are non-empty, and some owner sends exactly 8 to some trainer; which slots are non-empty varies. `cnt2`: equals the number of non-negative entries of the matching src2 slot.
All inputs are finite; a program needn't handle non-finite values.
Results may differ from the reference program's by a relative error of at most 0.00035.
The reference program's roundings to bfloat16 on the way count: a program that leaves them out, or rounds other values in their place, can miss the bound.
Values may be sent and summed in bfloat16 or wider, within the bound.
No kernel may reach another device: no remote copies, remote signals or barrier semaphores. Data moves between devices by JAX's collectives and lax.ppermute only.
A program may use at most 128 MiB of HBM per device.

```python
import math
import jax
import jax.numpy as jnp
from jax import lax

F = 128
H = 256
C = 172
FAN1 = 15
FAN2 = 10
STEP = 4
SEEDS = 2048
MID = 8192
CAP1 = 64
CAP2 = 16
LIVE1 = 32
LIVE2 = 8
PARAMS = 155648
N_DOM = 32


def graph_block(key, tag, slots, live_most, fanout, targets, sources):
    devices = N_DOM
    subkeys = jax.random.split(jax.random.fold_in(key, tag), 6)
    pair_id = jnp.arange(devices * devices, dtype=jnp.int32).reshape(devices, devices, 1)
    forced_pair = jax.random.randint(subkeys[0], (), 0, devices * devices)
    live_total = jax.random.randint(subkeys[1], (devices, devices, 1), max(1, live_most // 2), live_most + 1)
    live_total = jnp.where(pair_id == forced_pair, live_most, live_total)
    scores = jax.random.randint(subkeys[2], (devices, devices, slots), 0, slots) * slots + jnp.arange(slots, dtype=jnp.int32)[None, None, :]
    rank = jnp.argsort(jnp.argsort(scores, axis=2), axis=2).astype(jnp.int32)
    live_slot = rank < live_total
    slot_count = jnp.where(live_slot, jax.random.randint(subkeys[3], (devices, devices, slots), fanout // 2, fanout + 1), 0)
    slot_count = jnp.where((pair_id == forced_pair) & (rank == 0), fanout, slot_count)
    source_rows = jax.random.randint(subkeys[4], (devices, devices, slots, fanout), 0, sources)
    position = jnp.arange(fanout, dtype=jnp.int32)[None, None, None, :]
    source_rows = jnp.where(position < slot_count[..., None], source_rows, -1)
    target_rows = jax.random.randint(subkeys[5], (devices, devices, slots), 0, targets)
    return (slot_count, source_rows, target_rows)


def draw_src1(key, part):
    slot_count, source_rows, target_rows = graph_block(key, 11, CAP1, LIVE1, FAN1, MID, MID)
    return source_rows.reshape(-1, FAN1)


def draw_cnt1(key, part):
    slot_count, source_rows, target_rows = graph_block(key, 11, CAP1, LIVE1, FAN1, MID, MID)
    return slot_count.transpose(1, 0, 2).reshape(-1)


def draw_dst1(key, part):
    slot_count, source_rows, target_rows = graph_block(key, 11, CAP1, LIVE1, FAN1, MID, MID)
    return target_rows.transpose(1, 0, 2).reshape(-1)


def draw_src2(key, part):
    slot_count, source_rows, target_rows = graph_block(key, 23, CAP2, LIVE2, FAN2, SEEDS, MID)
    return source_rows.reshape(-1, FAN2)


def draw_cnt2(key, part):
    slot_count, source_rows, target_rows = graph_block(key, 23, CAP2, LIVE2, FAN2, SEEDS, MID)
    return slot_count.transpose(1, 0, 2).reshape(-1)


def draw_dst2(key, part):
    slot_count, source_rows, target_rows = graph_block(key, 23, CAP2, LIVE2, FAN2, SEEDS, MID)
    return target_rows.transpose(1, 0, 2).reshape(-1)


def draw_seed_count(key, part):
    subkeys = jax.random.split(jax.random.fold_in(key, 37), 2)
    counts = jax.random.randint(subkeys[0], (N_DOM,), SEEDS // 2, SEEDS + 1)
    forced_slot = jax.random.randint(subkeys[1], (), 0, N_DOM)
    return counts.at[forced_slot].set(SEEDS)


def draw_master(key, part):
    subkeys = jax.random.split(jax.random.fold_in(key, 41), 5)
    used = 2 * F * H + 2 * H * C + H + C
    pieces = [jax.random.normal(subkeys[0], (2 * F * H,), jnp.float32) * F ** (-0.5), jax.random.normal(subkeys[1], (2 * H * C,), jnp.float32) * H ** (-0.5), jax.random.normal(subkeys[2], (H,), jnp.float32) * 0.3, jax.random.normal(subkeys[3], (C,), jnp.float32) * 0.3, jax.random.normal(subkeys[4], (PARAMS - used,), jnp.float32) * 0.05]
    return jnp.concatenate(pieces).astype(jnp.float32)


def plant(array, stream_key, least, high):
    longest = array.shape.index(max(array.shape))
    spots = []
    for shift in (0, 1):
        where = [jax.random.randint(jax.random.fold_in(stream_key, axis), (), 0, length) for axis, length in enumerate(array.shape)]
        where[longest] = (where[longest] + shift) % array.shape[longest]
        spots.append(tuple(where))
    return array.at[spots[0]].set(least).at[spots[1]].set(high)


def level_of(rng, shape, cuts, smallest, largest):
    def one(dim, blocks):
        draws = jax.random.uniform(jax.random.fold_in(jax.random.fold_in(rng, 6), dim), (blocks,), jnp.float32, smallest / len(cuts), largest / len(cuts))
        return jnp.repeat(jnp.exp(draws), shape[dim] // blocks).reshape((-1,) + (1,) * (len(shape) - dim - 1))

    gain = one(*cuts[0])
    for cut in cuts[1:]:
        gain = gain * one(*cut)
    return gain


def scatter_about(rng, extent, spread, limit, shards=(), kind=jnp.bfloat16):
    entries = spread * jax.random.normal(rng, extent, jnp.float32)
    if shards:
        entries = entries * level_of(rng, extent, shards, -0.22, 0.18)
    return jnp.clip(entries, -limit, limit).astype(kind)


def setup_inputs(seed: int = 0) -> dict:
    seeds = jax.random.split(jax.random.key(seed), 13)
    features = scatter_about(seeds[0], (N_DOM * MID, F), 1.0, 6.0, ((0, 32),))
    labels = plant(jax.random.randint(seeds[1], (N_DOM * SEEDS,), 0, C), jax.random.fold_in(seeds[1], 1), 0, C - 1).astype(jnp.int32)
    seed_count = draw_seed_count(jax.random.fold_in(seeds[12], 71), 0)
    src1 = draw_src1(jax.random.fold_in(seeds[12], 71), 0)
    cnt1 = draw_cnt1(jax.random.fold_in(seeds[12], 71), 0)
    dst1 = draw_dst1(jax.random.fold_in(seeds[12], 71), 0)
    src2 = draw_src2(jax.random.fold_in(seeds[12], 71), 0)
    cnt2 = draw_cnt2(jax.random.fold_in(seeds[12], 71), 0)
    dst2 = draw_dst2(jax.random.fold_in(seeds[12], 71), 0)
    master = draw_master(jax.random.fold_in(seeds[12], 71), 0)
    moment1 = scatter_about(seeds[10], (PARAMS,), 0.003, 0.046875, ((0, 32),), jnp.float32)
    moment2 = jnp.clip(jnp.exp(math.log(0.0001) - 4.6051702 * jax.random.uniform(seeds[11], (PARAMS,), jnp.float32) ** level_of(seeds[11], (PARAMS,), ((0, 32),), -0.2, 0.2)), 9.999999974752427e-07, 0.0001)
    return {"features": features, "labels": labels, "seed_count": seed_count, "src1": src1, "cnt1": cnt1, "dst1": dst1, "src2": src2, "cnt2": cnt2, "dst2": dst2, "master": master, "moment1": moment1, "moment2": moment2}


highest = lax.Precision.HIGHEST
learn_rate = 0.02
weight_decay = 0.01
adam_eps = 1e-08

@jax.custom_vjp
def low(v):
    return lax.optimization_barrier(v.astype(jnp.bfloat16)).astype(jnp.float32)

@jax.custom_vjp
def low_back(v):
    return v

def low_keep(v):
    return (low(v), None)

def low_pass(kept, grad):
    return (grad,)

def back_keep(v):
    return (v, None)

def back_low(kept, grad):
    return (low(grad),)
low.defvjp(low_keep, low_pass)
low_back.defvjp(back_keep, back_low)

def owner_sums(source_rows, sources):
    present = (sources >= 0).astype(source_rows.dtype)
    picked = source_rows[jnp.maximum(sources, 0)]
    return jnp.einsum('sf,sfw->sw', present, picked, precision=highest)

def owner_pair(pair_args):
    return owner_sums(pair_args[0], pair_args[1])

def unpack(weights_flat):
    first_end = 2 * F * H
    second_end = first_end + 2 * H * C
    w_first = weights_flat[:first_end].reshape(2, F, H)
    w_second = weights_flat[first_end:second_end].reshape(2, H, C)
    bias_one = weights_flat[second_end:second_end + H]
    bias_two = weights_flat[second_end + H:second_end + H + C]
    return (w_first, w_second, bias_one, bias_two)

def smooth_loss(logits, labels):
    target = (labels[:, None] == jnp.arange(C, dtype=jnp.int32)[None, :]).astype(logits.dtype)
    return jax.nn.logsumexp(logits, axis=1) - 0.9 * lax.optimization_barrier(jnp.sum(logits * target, 1)) - 0.1 * lax.optimization_barrier(jnp.mean(logits, 1))

def forward(master, feat_float, means_one, valid_mask, seed_total, src2, seg_two, degree_two, labels):
    devices = N_DOM
    w_first, w_second, bias_one, bias_two = unpack(low(master))
    z_one = jnp.dot(feat_float, w_first[0], precision=highest) + jnp.dot(means_one, w_first[1], precision=highest) + bias_one
    hidden = low(low_back(jax.nn.relu(z_one)))
    owner_fn = jax.checkpoint(owner_pair)
    partial_two = low(lax.map(owner_fn, (hidden.reshape(devices, MID, H), src2.reshape(devices, devices * CAP2, FAN2))))
    partial_two = partial_two.reshape(devices, devices, CAP2, H).transpose(1, 0, 2, 3).reshape(-1, H)
    sums_two = low_back(jax.ops.segment_sum(partial_two, seg_two, devices * SEEDS))
    means_two = low(sums_two / degree_two[:, None])
    self_rows = hidden.reshape(devices, MID, H)[:, :SEEDS].reshape(-1, H)
    logits = low_back(jnp.dot(self_rows, w_second[0], precision=highest) + jnp.dot(means_two, w_second[1], precision=highest) + bias_two)
    return jnp.sum(smooth_loss(logits, labels) * valid_mask) / seed_total

def reference(features, labels, seed_count, src1, cnt1, dst1, src2, cnt2, dst2, master, moment1, moment2):
    devices = N_DOM
    feat_float = features.astype(jnp.float32)
    partial_one = low(lax.map(owner_pair, (feat_float.reshape(devices, MID, F), src1.reshape(devices, devices * CAP1, FAN1))))
    partial_one = partial_one.reshape(devices, devices, CAP1, F).transpose(1, 0, 2, 3).reshape(-1, F)
    seg_one = jnp.arange(devices * devices * CAP1, dtype=jnp.int32) // (devices * CAP1) * MID + dst1
    sums_one = jax.ops.segment_sum(partial_one, seg_one, devices * MID)
    degree_one = jnp.maximum(jax.ops.segment_sum(cnt1, seg_one, devices * MID), 1).astype(jnp.float32)
    means_one = low(sums_one / degree_one[:, None])
    seg_two = jnp.arange(devices * devices * CAP2, dtype=jnp.int32) // (devices * CAP2) * SEEDS + dst2
    degree_two = jnp.maximum(jax.ops.segment_sum(cnt2, seg_two, devices * SEEDS), 1).astype(jnp.float32)
    valid_mask = (jnp.arange(SEEDS, dtype=jnp.int32)[None, :] < seed_count[:, None]).reshape(-1).astype(jnp.float32)
    seed_total = jnp.sum(seed_count).astype(jnp.float32)

    def objective(weights):
        return forward(weights, feat_float, means_one, valid_mask, seed_total, src2, seg_two, degree_two, labels)
    loss_value, pullback = jax.vjp(objective, master)
    gradient, = pullback(jnp.ones((), jnp.float32))
    new_first = 0.5 * moment1 + 0.5 * gradient
    new_second = 0.5 * moment2 + 0.5 * gradient * gradient
    correction = 1.0 - 0.5 ** STEP
    new_master = master - learn_rate * (new_first / correction / (jnp.sqrt(new_second / correction) + adam_eps) + weight_decay * master)
    return (loss_value, new_master, new_first, new_second)
```

```python
import jax
import jax.numpy as jnp
from jax import lax
from jax.experimental import pallas as pl
from jax.experimental.pallas import tpu as pltpu
from jax.sharding import PartitionSpec as P

F = 128
H = 256
C = 172
STEP = 4
SEEDS = 2048
MID = 8192
CAP1 = 64
CAP2 = 16
LIVE1 = 32
LIVE2 = 8
FAN1 = 15
FAN2 = 10
L = 128
ROWS1 = 2 * F * H // L
ROWS2 = 2 * H * C // L
BIAS = ROWS1 + ROWS2
LEAD = 8

learn_rate = 0.02
weight_decay = 0.01
adam_eps = 1e-08
f32 = jnp.float32
bf16 = jnp.bfloat16
i32 = jnp.int32
VM = pl.BlockSpec(memory_space=pltpu.VMEM)
SM = pl.BlockSpec(memory_space=pltpu.SMEM)


def params(limit=48):
    return pltpu.CompilerParams(vmem_limit_bytes=limit * 2**20)


def cost(flops, nbytes):
    return pl.CostEstimate(flops=int(flops), bytes_accessed=int(nbytes), transcendentals=0)


def nn(a, b):
    return lax.dot_general(a, b, (((1,), (0,)), ((), ())), preferred_element_type=f32)


def nt(a, b):
    return lax.dot_general(a, b, (((1,), (1,)), ((), ())), preferred_element_type=f32)


def tn(a, b):
    return lax.dot_general(a, b, (((0,), (0,)), ((), ())), preferred_element_type=f32)


def iota(shape, dim, dtype=i32):
    return lax.broadcasted_iota(i32, shape, dim).astype(dtype)


def live_key(live, cap, keep):
    row = iota((256, 256), 0)
    col = iota((256, 256), 1)
    before = ((row < col) & (row // cap == col // cap)).astype(f32).astype(bf16)
    place = nn(live.astype(f32).astype(bf16), before)
    group = iota(live.shape, 1) // cap
    return jnp.where(live, place + (group * keep).astype(f32), -1.0)


def pick_matrix(key_row):
    return (key_row == iota((L, 256), 0, f32)).astype(f32).astype(bf16)


def split_pick(value, pick):
    hi = lax.shift_right_logical(value, 6)
    lo = lax.bitwise_and(value, 63)
    both = jnp.concatenate([hi, lo], axis=0).astype(f32).astype(bf16)
    got = nt(both, pick)
    n = value.shape[0]
    return got[:n] * 64.0 + got[n:]


def rows256(ref, g):
    return jnp.concatenate([ref[2 * g : 2 * g + 1, :], ref[2 * g + 1 : 2 * g + 2, :]], axis=1)


def stack256(ref, groups):
    return jnp.concatenate([rows256(ref, g) for g in range(groups)], axis=0)


def source_tables(src_ref, fan, cap, keep, offset, groups):
    live = jnp.concatenate([src_ref[0:1, 256 * g : 256 * g + 256] for g in range(groups)], axis=0) >= 0
    key = live_key(live, cap, keep)
    tables = []
    for g in range(groups):
        pick = pick_matrix(key[g : g + 1])
        block = src_ref[:, 256 * g : 256 * g + 256]
        block = jnp.where(block >= 0, block + offset, 0)
        block = jnp.concatenate([block, jnp.zeros((16 - fan, 256), i32)], axis=0)
        tables.append(split_pick(block, pick))
    return tables


def target_tables(cnt_ref, dst_ref, cap, keep, groups, dst_out, cnt_out):
    cnt = stack256(cnt_ref, groups)
    key = live_key(cnt > 0, cap, keep)
    for g in range(groups):
        pick = pick_matrix(key[g : g + 1])
        dst = jnp.broadcast_to(rows256(dst_ref, g), (8, 256))
        dst_out[:, L * g : L * g + L] = split_pick(dst, pick)
        reps = jnp.broadcast_to(cnt[g : g + 1].astype(f32), (L, 256)).astype(bf16)
        cnt_out[L * g : L * g + L, :] = nt(pick, reps).astype(bf16)


def prep_sources(src1_ref, src2_ref, idx_out, idx2_out):
    g1 = src1_ref.shape[1] // 256
    g2 = src2_ref.shape[1] // 256
    for g, t in enumerate(source_tables(src1_ref, FAN1, CAP1, LIVE1, LEAD, g1)):
        t = t.astype(i32)
        idx_out[:, L * g : L * g + L] = t[0:8] + t[8:16] * 65536
    for g, t in enumerate(source_tables(src2_ref, FAN2, CAP2, LIVE2, 1, g2)):
        idx2_out[:, L * g : L * g + L] = t - 1.0


def prep_targets(cnt1_ref, dst1_ref, cnt2_ref, dst2_ref, d1_out, c1_out, d2_out, c2_out):
    g1 = cnt1_ref.shape[0] // 2
    g2 = cnt2_ref.shape[0] // 2
    target_tables(cnt1_ref, dst1_ref, CAP1, LIVE1, g1, d1_out, c1_out)
    target_tables(cnt2_ref, dst2_ref, CAP2, LIVE2, g2, d2_out, c2_out)


def weight_rows(master_ref, count_ref, out_ref):
    rows = master_ref.shape[0]
    out_ref[...] = jnp.zeros(out_ref.shape, bf16)
    seeds = count_ref[0]
    hi = lax.shift_right_logical(seeds, 4).astype(f32)
    lo = lax.bitwise_and(seeds, 15).astype(f32)
    lane = iota((1, L), 1)
    extra = jnp.where(lane == 0, hi, jnp.where(lane == 1, lo, 0.0))
    block = jnp.concatenate([master_ref[...], extra], axis=0).astype(bf16)
    for d in range(out_ref.shape[0]):
        out_ref[d, 0 : rows + 1, :] = block


def gather_sums(idx_ref, feat_ref, out_ref, table, hold):
    table[0:LEAD, :] = jnp.zeros((LEAD, F), f32)

    def widen(i, carry):
        at = pl.multiple_of(i * 512, 512)
        table[pl.ds(at + LEAD, 512), :] = feat_ref[pl.ds(at, 512), :].astype(f32)
        return carry

    lax.fori_loop(0, MID // 512, widen, 0)

    def sixteen(i, carry):
        at = pl.multiple_of(i * 16, 16)
        for u in range(16):
            picked = []
            for j in range(8):
                word = idx_ref[j, at + u]
                picked.append(table[pl.ds(lax.bitwise_and(word, 65535), 1), :])
                if j < 7:
                    picked.append(table[pl.ds(lax.shift_right_logical(word, 16), 1), :])
            while len(picked) > 1:
                picked = [a + b for a, b in zip(picked[::2], picked[1::2])] + picked[len(picked) // 2 * 2 :]
            hold[u : u + 1, :] = picked[0]
        out_ref[pl.ds(at, 16), :] = hold[...].astype(bf16)
        return carry

    lax.fori_loop(0, out_ref.shape[0] // 16, sixteen, 0)


def roll_left(x, r):
    return pltpu.roll(x, L - r, 1) if r else x


def unpack(rows, got_ref, w1_ref, b1_ref, w2_ref, b2_ref, total_ref, flat, left, right):
    devices = got_ref.shape[0]
    lane = iota((1, L), 1)
    seeds = jnp.zeros((1, L), f32)
    for d in range(devices):
        flat[d * rows : d * rows + rows, :] = got_ref[d, 0:rows, :].astype(f32)
        seeds = seeds + got_ref[d, rows : rows + 1, :].astype(f32)
    weight = jnp.where(lane == 0, 16.0, jnp.where(lane == 1, 1.0, 0.0))
    total = jnp.sum(seeds * weight, axis=1, keepdims=True)
    total_ref[...] = jnp.broadcast_to(total, total_ref.shape)
    w1_ref[:, 0:L] = flat[pl.ds(0, 256, stride=2), :].astype(bf16)
    w1_ref[:, L : 2 * L] = flat[pl.ds(1, 256, stride=2), :].astype(bf16)
    lanes = iota((16, L), 1)
    for i in range(32):
        q, r = divmod(C * i, L)
        one = roll_left(flat[pl.ds(ROWS1 + q, 16, stride=43), :], r)
        two = roll_left(flat[pl.ds(ROWS1 + q + 1, 16, stride=43), :], r)
        left[pl.ds(i, 16, stride=32), :] = jnp.where(lanes < L - r, one, two) if r else one
        tail = two
        if r + C - L > L:
            three = roll_left(flat[pl.ds(ROWS1 + q + 2, 16, stride=43), :], r)
            tail = jnp.where(lanes < L - r, two, three)
        right[pl.ds(i, 16, stride=32), :] = jnp.where(lanes < C - L, tail, 0.0)
    w2_ref[:, 0:L] = left[...].astype(bf16)
    w2_ref[:, L : 2 * L] = right[...].astype(bf16)
    b1 = jnp.concatenate([flat[BIAS : BIAS + 1, :], flat[BIAS + 1 : BIAS + 2, :]], axis=1)
    b1_ref[...] = jnp.broadcast_to(b1, b1_ref.shape)
    tail = jnp.where(lane < C - L, flat[BIAS + 3 : BIAS + 4, :], 0.0)
    b2 = jnp.concatenate([flat[BIAS + 2 : BIAS + 3, :], tail], axis=1)
    b2_ref[...] = jnp.broadcast_to(b2, b2_ref.shape)


def one_hot(row, start, count):
    near = (row - start.astype(f32)).astype(bf16)
    return (near == iota((count, row.shape[1]), 0, f32).astype(bf16)).astype(f32).astype(bf16)


def source_counts(idx_ref, start, count):
    total = one_hot(idx_ref[0:1, :], start, count)
    for j in range(1, FAN2):
        total = total + one_hot(idx_ref[j : j + 1, :], start, count)
    return total


def first_layer(
    feat_ref, sums_ref, cnt_ref, dst_ref, idx2_ref, w1_ref, b1_ref, pair_ref, act_ref, spread_ref, part_ref, right, acc
):
    step = pl.program_id(0)
    block = feat_ref.shape[0]

    @pl.when(step == 0)
    def _():
        right[:, 0:F] = sums_ref[...]
        right[:, F : 2 * F] = cnt_ref[...]
        acc[...] = jnp.zeros(acc.shape, f32)

    for k in range(block // 256):
        start = step * block + k * 256
        here = slice(k * 256, k * 256 + 256)
        got = nn(one_hot(dst_ref[0:1, :], start, 256), right[...])
        mean = (got[:, 0:F] / jnp.maximum(got[:, F : 2 * F], 1.0)).astype(bf16)
        pair = jnp.concatenate([feat_ref[here, :], mean], axis=1)
        pair_ref[here, :] = pair
        act = jnp.maximum(nn(pair, w1_ref[...]) + b1_ref[0:1, :], 0.0).astype(bf16)
        act_ref[here, :] = act
        spread = source_counts(idx2_ref, start, 256)
        spread_ref[here, :] = spread
        acc[...] += tn(spread, act)

    @pl.when(step == pl.num_programs(0) - 1)
    def _():
        part_ref[...] = acc[...].astype(bf16)


def second_layer(
    live_ref, labels_ref, act_ref, part_ref, cnt_ref, dst_ref, w2_ref, b2_ref, total_ref,
    ret_ref, grad_ref, mean_ref, loss_ref, acc, right,
):
    right[:, 0:H] = part_ref[...]
    right[:, H : H + L] = cnt_ref[...]
    acc[...] = jnp.zeros(acc.shape, f32)
    lane = iota((256, H), 1)
    real = lane < C
    total = total_ref[0:1, 0:1]
    loss = jnp.zeros((1, 1), f32)
    for k in range(SEEDS // 256):
        here = slice(k * 256, k * 256 + 256)
        hot = one_hot(dst_ref[0:1, :], jnp.int32(k * 256), 256)
        got = nn(hot, right[...])
        degree = jnp.maximum(got[:, H : H + L], 1.0)
        degree = jnp.concatenate([degree, degree], axis=1)
        mean = (got[:, 0:H] / degree).astype(bf16)
        mean_ref[here, :] = mean
        logits = nn(act_ref[here, :], w2_ref[0:H, :]) + nn(mean, w2_ref[H : 2 * H, :]) + b2_ref[0:1, :]
        top = jnp.max(jnp.where(real, logits, -3e38), axis=1, keepdims=True)
        raised = jnp.where(real, jnp.exp(jnp.where(real, logits - top, 0.0)), 0.0)
        norm = jnp.sum(raised, axis=1, keepdims=True)
        label = jnp.transpose(jnp.broadcast_to(rows256(labels_ref, k).astype(f32), (8, 256)))[:, 0:1]
        target = jnp.where(lane.astype(f32) == label, 1.0, 0.0)
        valid = (iota((256, 1), 0) + k * 256 < live_ref[0]).astype(f32)
        ce = (
            top + jnp.log(norm)
            - 0.9 * jnp.sum(logits * target, axis=1, keepdims=True)
            - 0.1 * (jnp.sum(jnp.where(real, logits, 0.0), axis=1, keepdims=True) / C)
        )
        loss = loss + jnp.sum(ce * valid, axis=0, keepdims=True)
        grad = jnp.where(real, (raised / norm - 0.9 * target - 0.1 / C) * (valid / total), 0.0).astype(bf16)
        grad_ref[here, :] = grad
        back = (nt(grad, w2_ref[H : 2 * H, :]) / degree).astype(bf16)
        acc[...] += tn(hot, back)
    ret_ref[...] = acc[...].astype(bf16)
    loss_ref[...] = jnp.broadcast_to(loss, loss_ref.shape)


def second_grads(act_ref, mean_ref, grad_ref, w2_ref, self_ref, flat_ref, left, right):
    grad = grad_ref[...]
    for part, rows in ((0, act_ref), (1, mean_ref)):
        got = tn(rows[...], grad)
        left[part * H : part * H + H, :] = got[:, 0:L]
        right[part * H : part * H + H, :] = got[:, L : 2 * L]
    self_ref[...] = nt(grad, w2_ref[0:H, :])
    lanes = iota((16, L), 1)
    for m in range(43):
        i, c = divmod(L * m, C)
        a0 = roll_left(left[pl.ds(i, 16, stride=32), :], c) if c < L else None
        a1 = roll_left(right[pl.ds(i, 16, stride=32), :], c % L)
        piece = a1 if a0 is None else (jnp.where(lanes < L - c, a0, a1) if c else a0)
        held = C - c
        if held < L:
            nxt = left[pl.ds(i + 1, 16, stride=32), :]
            piece = jnp.where(lanes < held, piece, pltpu.roll(nxt, held, 1) if held else nxt)
        flat_ref[pl.ds(m, 16, stride=43), :] = piece
    bias = jnp.sum(grad.astype(f32), axis=0, keepdims=True)
    flat_ref[ROWS2 : ROWS2 + 1, :] = bias[:, 0:L]
    flat_ref[ROWS2 + 1 : ROWS2 + 2, :] = bias[:, L : 2 * L]
    flat_ref[ROWS2 + 2 :, :] = jnp.zeros((flat_ref.shape[0] - ROWS2 - 2, L), f32)


def first_grads(
    rows, pair_ref, act_ref, spread_ref, slot_ref, self_ref, flat2_ref, loss_ref, out_ref, acc, bias, flat
):
    step = pl.program_id(0)
    block = pair_ref.shape[0]

    @pl.when(step == 0)
    def _():
        acc[...] = jnp.zeros(acc.shape, f32)
        bias[...] = jnp.zeros(bias.shape, f32)

    seeded = jnp.where(step * block < SEEDS, 1.0, 0.0)
    d_act = nn(spread_ref[...], slot_ref[...]) + self_ref[...] * seeded
    d_act = jnp.where(act_ref[...].astype(f32) > 0, d_act.astype(bf16).astype(f32), 0.0)
    bias[...] += jnp.sum(d_act.reshape(block // 8, 8, H), axis=0)
    acc[...] += tn(pair_ref[...], d_act.astype(bf16))

    @pl.when(step == pl.num_programs(0) - 1)
    def _():
        flat[pl.ds(0, 256, stride=2), :] = acc[:, 0:L]
        flat[pl.ds(1, 256, stride=2), :] = acc[:, L : 2 * L]
        flat[ROWS1:BIAS, :] = flat2_ref[0:ROWS2, :]
        b1 = jnp.sum(bias[...], axis=0, keepdims=True)
        flat[BIAS : BIAS + 1, :] = b1[:, 0:L]
        flat[BIAS + 1 : BIAS + 2, :] = b1[:, L : 2 * L]
        flat[BIAS + 2 : BIAS + 4, :] = flat2_ref[ROWS2 : ROWS2 + 2, :]
        flat[BIAS + 4 :, :] = jnp.zeros((flat.shape[0] - BIAS - 4, L), f32)
        spare = out_ref.shape[1] - rows
        for d in range(out_ref.shape[0]):
            out_ref[d, 0:rows, :] = flat[d * rows : d * rows + rows, :]
            out_ref[d, rows:, :] = loss_ref[0:spare, :]


def adamw(rows, got_ref, total_ref, master_ref, m1_ref, m2_ref, loss_ref, new_ref, n1_ref, n2_ref):
    total = jnp.sum(got_ref[...], axis=0)
    grad = total[0:rows]
    loss_ref[...] = total[rows : rows + 1] / total_ref[0:1, :]
    first = 0.5 * m1_ref[...] + 0.5 * grad
    second = 0.5 * m2_ref[...] + 0.5 * grad * grad
    fix = 1.0 - 0.5**STEP
    master = master_ref[...]
    n1_ref[...] = first
    n2_ref[...] = second
    new_ref[...] = master - learn_rate * (
        first / fix / (jnp.sqrt(second / fix) + adam_eps) + weight_decay * master
    )


def ceil_to(n, k):
    return -(-n // k) * k


def exchange(x):
    return lax.all_to_all(x, "dom", split_axis=0, concat_axis=0, tiled=True)


def body(features, labels, seed_count, src1, cnt1, dst1, src2, cnt2, dst2, master, moment1, moment2):
    devices = lax.axis_size("dom")
    rows = master.shape[0] // L
    n1 = devices * LIVE1
    n2 = devices * LIVE2
    send_rows = ceil_to(rows + 1, 16)
    back_rows = ceil_to(rows + 1, 8)
    S = jax.ShapeDtypeStruct
    call = pl.pallas_call
    master2 = master.reshape(rows, L)
    w_send = call(
        weight_rows, out_shape=S((devices, send_rows, L), bf16), in_specs=[VM, SM], out_specs=VM,
        compiler_params=params(), name="weight_rows",
    )(master2, seed_count)
    w_got = exchange(w_send)
    idx1, idx2 = call(
        prep_sources, out_shape=(S((8, n1), i32), S((16, n2), f32)), in_specs=[VM, VM], out_specs=(VM, VM),
        compiler_params=params(), name="prep_sources", cost_estimate=cost(1e7, 2e5),
    )(src1.T, src2.T)
    sums = call(
        gather_sums, out_shape=S((n1, F), bf16), in_specs=[SM, VM], out_specs=VM,
        scratch_shapes=[pltpu.VMEM((MID + LEAD, F), f32), pltpu.VMEM((16, F), f32)],
        compiler_params=params(), name="gather_sums", cost_estimate=cost(2e9, 4e7),
    )(idx1, features)
    got1 = exchange(sums.reshape(devices, LIVE1, F)).reshape(n1, F)
    dst1c, cnt1c, dst2c, cnt2c = call(
        prep_targets,
        out_shape=(S((8, n1), f32), S((n1, L), bf16), S((8, n2), f32), S((n2, L), bf16)),
        in_specs=[VM] * 4, out_specs=(VM,) * 4, compiler_params=params(), name="prep_targets",
        cost_estimate=cost(1e7, 4e5),
    )(*(a.reshape(-1, L) for a in (cnt1, dst1, cnt2, dst2)))
    w1, b1, w2, b2, total = call(
        lambda *refs: unpack(rows, *refs),
        out_shape=(S((256, H), bf16), S((8, H), f32), S((2 * H, H), bf16), S((8, H), f32), S((8, L), f32)),
        in_specs=[VM], out_specs=(VM,) * 5,
        scratch_shapes=[pltpu.VMEM((devices * rows, L), f32), pltpu.VMEM((2 * H, L), f32), pltpu.VMEM((2 * H, L), f32)],
        compiler_params=params(), name="unpack", cost_estimate=cost(1e7, 1e6),
    )(w_got)
    block = 1024
    steps = MID // block
    whole = lambda *shape: pl.BlockSpec(shape, lambda i: (0,) * len(shape))
    part = lambda width: pl.BlockSpec((block, width), lambda i: (i, 0))
    pair, act, spread, part2 = call(
        first_layer, grid=(steps,),
        out_shape=(S((MID, 2 * F), bf16), S((MID, H), bf16), S((MID, n2), bf16), S((n2, H), bf16)),
        in_specs=[part(F), whole(n1, F), whole(n1, L), whole(8, n1), whole(16, n2), whole(2 * F, H), whole(8, H)],
        out_specs=(part(2 * F), part(H), part(n2), whole(n2, H)),
        scratch_shapes=[pltpu.VMEM((n1, 2 * F), bf16), pltpu.VMEM((n2, H), f32)],
        compiler_params=params(), name="first_layer", cost_estimate=cost(8e9, 2e7),
    )(features, got1, cnt1c, dst1c, idx2, w1, b1)
    got2 = exchange(part2.reshape(devices, LIVE2, H)).reshape(n2, H)
    seeds_only = pl.BlockSpec((SEEDS, H), lambda i: (0, 0))
    ret, grad, mean2, loss = call(
        second_layer, grid=(1,),
        out_shape=(S((n2, H), bf16), S((SEEDS, H), bf16), S((SEEDS, H), bf16), S((8, L), f32)),
        in_specs=[SM, whole(SEEDS // L, L), seeds_only, whole(n2, H), whole(n2, L), whole(8, n2), whole(2 * H, H),
                  whole(8, H), whole(8, L)],
        out_specs=(whole(n2, H), whole(SEEDS, H), whole(SEEDS, H), whole(8, L)),
        scratch_shapes=[pltpu.VMEM((n2, H), f32), pltpu.VMEM((n2, H + L), bf16)],
        compiler_params=params(), name="second_layer", cost_estimate=cost(4e9, 5e6),
    )(seed_count, labels.reshape(-1, L), act, got2, cnt2c, dst2c, w2, b2, total)
    slot = exchange(ret.reshape(devices, LIVE2, H)).reshape(n2, H)
    from_self, flat2 = call(
        second_grads, grid=(1,), out_shape=(S((SEEDS, H), f32), S((ROWS2 + 16, L), f32)),
        in_specs=[seeds_only, whole(SEEDS, H), whole(SEEDS, H), whole(2 * H, H)],
        out_specs=(whole(SEEDS, H), whole(ROWS2 + 16, L)),
        scratch_shapes=[pltpu.VMEM((2 * H, L), f32), pltpu.VMEM((2 * H, L), f32)],
        compiler_params=params(), name="second_grads", cost_estimate=cost(4e9, 5e6),
    )(act, mean2, grad, w2)
    last = SEEDS // block - 1
    out = call(
        lambda *refs: first_grads(rows, *refs), grid=(steps,), out_shape=S((devices, back_rows, L), f32),
        in_specs=[part(2 * F), part(H), part(n2), whole(n2, H),
                  pl.BlockSpec((block, H), lambda i: (jnp.minimum(i, last), 0)), whole(ROWS2 + 16, L), whole(8, L)],
        out_specs=whole(devices, back_rows, L),
        scratch_shapes=[pltpu.VMEM((2 * F, H), f32), pltpu.VMEM((8, H), f32), pltpu.VMEM((devices * rows, L), f32)],
        compiler_params=params(), name="first_grads", cost_estimate=cost(4e9, 1e7),
    )(pair, act, spread, slot, from_self, flat2, loss)
    got3 = exchange(out)
    vec = S((rows, L), f32)
    loss_row, new_master, new_first, new_second = call(
        lambda *refs: adamw(rows, *refs), out_shape=(S((1, L), f32), vec, vec, vec), in_specs=[VM] * 5,
        out_specs=(VM,) * 4, compiler_params=params(), name="adamw",
    )(got3, total, master2, moment1.reshape(rows, L), moment2.reshape(rows, L))
    return (loss_row[0, 0], new_master.reshape(-1), new_first.reshape(-1), new_second.reshape(-1))


def solution(mesh):
    placed = (
        P("dom", None),
        P("dom"),
        P("dom"),
        P("dom", None),
        P("dom"),
        P("dom"),
        P("dom", None),
        P("dom"),
        P("dom"),
        P("dom"),
        P("dom"),
        P("dom"),
    )
    return jax.shard_map(
        body,
        mesh=mesh,
        in_specs=placed,
        out_specs=(P(), P("dom"), P("dom"), P("dom")),
        check_vma=False,
    )
```
